32 devices in a mesh: samples: 8 (over z, y), snps: 4 (over x, core).
Axes of the slice: x: 2, y: 2, z: 4, core: 2. Of those that a mesh axis runs over, the one named last changes fastest.
Arguments:
- genotype: int32 [4096, 1536], P('samples', 'snps'), may hold values from 0 to 2
- mask: int32 [4096, 1536], P('samples', 'snps'), may hold values 0 or 1
Outputs:
- blocks: float32 [4096, 2560], P('samples', 'snps')
The draws below stay inside these ranges and needn't reach their ends.
All inputs are finite; a program needn't handle non-finite values. No bound on the sum of `mask` on one device may be relied on, other than what follows from the above.
Results may differ from the reference program's by a relative error of at most 0.0014.
Values may be sent and summed in bfloat16 or wider, within the bound.
A program may use at most 128 MiB of HBM per device.

```python
import jax
import jax.numpy as jnp
from jax import lax

SNPS = 1536
SAMPLE_DEV = 512
SAMPLES = 4096
OFFSETS = 5
N_SAMPLES = 8


def draw_genotype(key, part):
    base_key = jax.random.fold_in(key, 11)
    key_percent = jax.random.fold_in(base_key, 1)
    key_first = jax.random.fold_in(base_key, 2)
    key_second = jax.random.fold_in(base_key, 3)
    percent = jax.random.randint(key_percent, (1, SNPS), 5, 31)
    sample_rows = lax.broadcasted_iota(jnp.int32, (SAMPLES, 1), 0)
    limit = percent * (SAMPLES + 2 * sample_rows)
    first_allele = jax.random.randint(key_first, (SAMPLES, SNPS), 0, 100) * SAMPLES
    second_allele = jax.random.randint(key_second, (SAMPLES, SNPS), 0, 100) * SAMPLES
    return (first_allele < limit).astype(jnp.int32) + (second_allele < limit).astype(jnp.int32)


def place_ends(values, rng, smallest, top_value):
    dims = values.shape
    place = [jax.random.randint(jax.random.fold_in(rng, axis), (), 0, dims[axis]) for axis in range(len(dims))]
    values = values.at[tuple(place)].set(smallest)
    longest = dims.index(max(dims))
    place[longest] = (place[longest] + 1) % dims[longest]
    return values.at[tuple(place)].set(top_value)


def setup_inputs(seed: int = 0) -> dict:
    splits = jax.random.split(jax.random.key(seed), 3)
    genotype = draw_genotype(jax.random.fold_in(splits[2], 71), 0)
    mask = place_ends((jax.random.randint(splits[1], (SAMPLES, SNPS), 0, 10) < 9).astype(jnp.int32), jax.random.fold_in(splits[1], 1), 0, 1)
    return dict(genotype=genotype, mask=mask)


def standardize(genotype, mask):
    dosage = genotype.astype(jnp.float32)
    observed_mask = mask.astype(jnp.float32)
    allele_sum = lax.optimization_barrier(jnp.sum(dosage * observed_mask, axis=0))
    observed_sum = lax.optimization_barrier(jnp.sum(observed_mask, axis=0))
    frequency = (allele_sum + 1.0) / (2.0 * observed_sum + 2.0)
    scaled = observed_mask * (dosage - 2.0 * frequency) / jnp.sqrt(2.0 * frequency * (1.0 - frequency))
    return scaled.astype(jnp.bfloat16)

def reference(genotype, mask):
    standard = standardize(genotype, mask)

    def block_row(block_index):
        begin = (block_index * SAMPLE_DEV).astype(jnp.int32)
        own_rows = lax.dynamic_slice_in_dim(standard, begin, SAMPLE_DEV, 0)
        rolled = jnp.roll(standard, -begin, axis=0)[:OFFSETS * SAMPLE_DEV]
        product = lax.dot_general(own_rows, rolled, (((1,), (1,)), ((), ())), preferred_element_type=jnp.float32)
        return product / SNPS
    result = lax.map(block_row, jnp.arange(N_SAMPLES, dtype=jnp.int32))
    return result.reshape(SAMPLES, OFFSETS * SAMPLE_DEV)
```

```python
import math

import jax
import jax.numpy as jnp
from jax import lax
from jax.sharding import PartitionSpec as P


def standardize(dosage, observed_mask, allele_sum, observed_sum):
    frequency = (allele_sum + 1.0) / (2.0 * observed_sum + 2.0)
    scaled = (
        observed_mask * (dosage - 2.0 * frequency) / jnp.sqrt(2.0 * frequency * (1.0 - frequency))
    )
    return scaled.astype(jnp.bfloat16)


def cross_block(own_rows, other_rows):
    return lax.dot_general(
        own_rows, other_rows, (((1,), (1,)), ((), ())), preferred_element_type=jnp.float32
    )


def rows_for_columns(full_rows, offsets):
    circle_size = lax.axis_size("samples")
    parts = lax.axis_size("snps")
    block_rows = full_rows.shape[0]
    width = offsets * block_rows // parts
    piece = math.gcd(block_rows, width)
    per_block = block_rows // piece
    per_part = width // piece
    part = lax.axis_index("snps")
    pieces = []
    for index in range(per_part):
        sub = (part * per_part + index) % per_block
        sent = lax.dynamic_slice_in_dim(full_rows, sub * piece, piece, axis=0)
        pairs = []
        for row in range(circle_size):
            for column in range(parts):
                ahead = (column * per_part + index) // per_block
                source = (row + ahead) % circle_size
                pairs.append((source * parts + column, row * parts + column))
        pieces.append(lax.ppermute(sent, ("samples", "snps"), pairs))
    return jnp.concatenate(pieces, axis=0)


def per_device(genotype, mask):
    dosage = genotype.astype(jnp.float32)
    observed_mask = mask.astype(jnp.float32)
    allele_sum, observed_sum = lax.psum(
        (jnp.sum(dosage * observed_mask, axis=0), jnp.sum(observed_mask, axis=0)), "samples"
    )
    standard = standardize(dosage, observed_mask, allele_sum, observed_sum)
    offsets = lax.axis_size("samples") // 2 + 1
    full_rows = lax.all_gather(standard, "snps", axis=1, tiled=True)
    others = rows_for_columns(full_rows, offsets)
    return cross_block(full_rows, others) / full_rows.shape[1]


def solution(mesh):
    return jax.shard_map(
        per_device,
        mesh=mesh,
        in_specs=(P("samples", "snps"), P("samples", "snps")),
        out_specs=P("samples", "snps"),
        check_vma=False,
    )
```
